32 devices in a mesh: pb: 8 (over z, x), ka: 4 (over y, core).
Axes of the slice: x: 2, y: 2, z: 4, core: 2. Of those that a mesh axis runs over, the one named last changes fastest.
Arguments:
- queries: bfloat16 [4096, 128], P('pb'), may hold values from -96 to 96
- keys: bfloat16 [32768, 128], P('ka'), may hold values from -4 to 4
- values: bfloat16 [32768, 128], P('ka'), may hold values from -6 to 6
- bias: float32 [32768], P(('pb', 'ka')), may hold values from -6 to 6
- grad_out: bfloat16 [4096, 128], P('pb'), may hold values from -1536 to 1536
- group_start: int32 [1], replicated, may hold values from 8192 to 28672
Outputs:
- query_grad: bfloat16 [4096, 128], P(('pb', 'ka'))
- key_grad: bfloat16 [32768, 128], P(('ka', 'pb'))
- value_grad: bfloat16 [32768, 128], P(('ka', 'pb'))
- bias_grad: float32 [32768], P(('pb', 'ka'))
The draws below stay inside these ranges and needn't reach their ends.
All inputs are finite; a program needn't handle non-finite values.
Results may differ from the reference program's by a relative error of at most 0.015.
Values may be sent and summed in bfloat16 or wider, within the bound.
A program may use at most 128 MiB of HBM per device.

```python
import jax
import jax.numpy as jnp
from jax import lax

D = 128
K_DEV = 8192
Q_LEN = 4096
K_LEN = 32768
BIAS = 32768


def base_keys(key):
    return jnp.clip(jax.random.normal(jax.random.fold_in(key, 23), (K_LEN, D), jnp.float32), -4.0, 4.0)


def draw_keys(key, part):
    key_table = base_keys(key)
    return key_table.astype(jnp.bfloat16)


def draw_queries(key, part):
    query_table = jnp.clip(jax.random.normal(jax.random.fold_in(key, 37), (Q_LEN, D), jnp.float32), -4.0, 4.0)
    return query_table.astype(jnp.bfloat16)


def levels(rng, dims, cuts, smallest, largest):
    factor_of = 1.0
    for position, parts in cuts:
        draws = jax.random.uniform(jax.random.fold_in(jax.random.fold_in(rng, 6), position), (parts,), jnp.float32, smallest / len(cuts), largest / len(cuts))
        factor_of = factor_of * jnp.repeat(jnp.exp(draws), dims[position] // parts).reshape((-1,) + (1,) * (len(dims) - 1 - position))
    return factor_of


def normal_values(stream_key, shape, deviation, bound, cuts=(), kind=jnp.bfloat16):
    entries = deviation * jax.random.normal(stream_key, shape, jnp.float32)
    if cuts:
        entries = entries * levels(stream_key, shape, cuts, -0.22, 0.18)
    return jnp.clip(entries, -bound, bound).astype(kind)


def setup_inputs(seed: int = 0) -> dict:
    key_list = jax.random.split(jax.random.key(seed), 7)
    queries = draw_queries(jax.random.fold_in(key_list[6], 71), 0)
    keys = draw_keys(jax.random.fold_in(key_list[6], 71), 0)
    values = normal_values(key_list[2], (K_LEN, D), 1.0, 6.0, ((0, 4),))
    bias = normal_values(key_list[3], (BIAS,), 1.0, 6.0, ((0, 32),), jnp.float32)
    grad_out = normal_values(key_list[4], (Q_LEN, D), 256.0, 1536.0, ((0, 8),))
    group_start = jax.random.randint(key_list[5], (1,), K_DEV, K_LEN - Q_LEN + 1).astype(jnp.int32)
    return dict(queries=queries, keys=keys, values=values, bias=bias, grad_out=grad_out, group_start=group_start)


negative = -1.0e30


def reference(queries, keys, values, bias, grad_out, group_start):
    score_scale = D ** -0.5
    block_size = min(256, Q_LEN)
    block_count = Q_LEN // block_size
    key_pos = jnp.arange(K_LEN, dtype=jnp.int32)
    group_first = group_start[0].astype(jnp.int32)

    def one_block(running, block_id):
        key_acc, value_acc, bias_acc = running
        first_row = (block_id * block_size).astype(jnp.int32)
        query_block = lax.dynamic_slice_in_dim(queries, first_row, block_size, 0)
        grad_block = lax.dynamic_slice_in_dim(grad_out, first_row, block_size, 0)
        query_pos = group_first + first_row + jnp.arange(block_size, dtype=jnp.int32)
        offsets = query_pos[:, None] - key_pos[None, :]
        visible = offsets >= 0
        place_at = jnp.where(visible, offsets, 0)
        scores = jnp.dot(query_block, keys.T, preferred_element_type=jnp.float32) * score_scale + bias[place_at]
        row_max = jnp.max(jnp.where(visible, scores, negative), axis=1)
        weights = jnp.where(visible, jnp.exp(scores - row_max[:, None]), 0.0)
        row_sum = jnp.sum(weights, axis=1)
        output = jnp.dot(weights.astype(jnp.bfloat16), values, preferred_element_type=jnp.float32) / row_sum[:, None]
        log_norm = row_max + jnp.log(row_sum)
        row_dots = jnp.sum(grad_block.astype(jnp.float32) * output, axis=1)
        prob_mat = jnp.where(visible, jnp.exp(scores - log_norm[:, None]), 0.0)
        dprob_mat = jnp.dot(grad_block, values.T, preferred_element_type=jnp.float32)
        dscore_mat = prob_mat * (dprob_mat - row_dots[:, None])
        dscore_low = dscore_mat.astype(jnp.bfloat16)
        query_part = jnp.dot(dscore_low, keys, preferred_element_type=jnp.float32) * score_scale
        key_acc = key_acc + jnp.dot(dscore_low.T, query_block, preferred_element_type=jnp.float32)
        value_acc = value_acc + jnp.dot(prob_mat.astype(jnp.bfloat16).T, grad_block, preferred_element_type=jnp.float32)
        slots = jnp.where(visible, offsets, BIAS).reshape(-1).astype(jnp.int32)
        bias_acc = bias_acc + jax.ops.segment_sum(dscore_mat.reshape(-1), slots, num_segments=BIAS + 1)[:BIAS]
        return (key_acc, value_acc, bias_acc), query_part.astype(jnp.bfloat16)

    start_state = (jnp.zeros((K_LEN, D), jnp.float32), jnp.zeros((K_LEN, D), jnp.float32), jnp.zeros((BIAS,), jnp.float32))
    final_state, query_parts = lax.scan(one_block, start_state, jnp.arange(block_count, dtype=jnp.int32))
    key_acc, value_acc, bias_acc = final_state
    query_grad = query_parts.reshape(Q_LEN, D)
    return query_grad, (key_acc * score_scale).astype(jnp.bfloat16), value_acc.astype(jnp.bfloat16), bias_acc
```

```python
import math

import jax
import jax.numpy as jnp
from jax import lax
from jax.experimental import pallas as pl
from jax.experimental.pallas import tpu as pltpu
from jax.sharding import PartitionSpec as P

LANES = 128
NEGATIVE = -1e30
FLOOR = -1e20
LOG2E = math.log2(math.e)
MESH = pl.DeviceIdType.MESH
VMEM = pl.BlockSpec(memory_space=pltpu.VMEM)


def dot_nt(a, b):
    return lax.dot_general(a, b, (((1,), (1,)), ((), ())), preferred_element_type=jnp.float32)


def dot_nn(a, b):
    return jnp.dot(a, b, preferred_element_type=jnp.float32)


def me_and_count(pb_size, ka_size):
    return lax.axis_index("pb") * ka_size + lax.axis_index("ka"), pb_size * ka_size


def peer_id(linear, ka_size):
    return (linear // ka_size, lax.rem(linear, ka_size))


def greet_all(me, count, ka_size):
    barrier = pltpu.get_barrier_semaphore()
    for k in range(1, count):
        pl.semaphore_signal(
            barrier, inc=1, device_id=peer_id(lax.rem(me + k, count), ka_size), device_id_type=MESH
        )
    pl.semaphore_wait(barrier, count - 1)


def push_all(src_of, dst_ref, send_sems, recv_sems, me, count, ka_size):
    copies = []
    for k in range(1, count):
        peer = lax.rem(me + k, count)
        copy = pltpu.make_async_remote_copy(
            src_ref=src_of(peer),
            dst_ref=dst_ref.at[me],
            send_sem=send_sems.at[k],
            recv_sem=recv_sems.at[k],
            device_id=peer_id(peer, ka_size),
            device_id_type=MESH,
        )
        copy.start()
        copies.append(copy)
    return copies


def gather_kernel(pb_size, ka_size, x_ref, out_ref, send_sems, recv_sems):
    me, count = me_and_count(pb_size, ka_size)
    greet_all(me, count, ka_size)
    copies = push_all(lambda peer: x_ref, out_ref, send_sems, recv_sems, me, count, ka_size)
    out_ref[me] = x_ref[...]
    for copy in copies:
        copy.wait()


def gather_small(x, pb_size, ka_size, collective_id):
    count = pb_size * ka_size
    return pl.pallas_call(
        lambda *refs: gather_kernel(pb_size, ka_size, *refs),
        out_shape=jax.ShapeDtypeStruct((count,) + x.shape, x.dtype),
        in_specs=[VMEM],
        out_specs=VMEM,
        scratch_shapes=[pltpu.SemaphoreType.DMA((count,)), pltpu.SemaphoreType.DMA((count,))],
        compiler_params=pltpu.CompilerParams(collective_id=collective_id, has_side_effects=True),
        name=f"gather_{collective_id}",
    )(x)


def entry_kernel(
    pb_size, ka_size, bias_ref, rows_ref, bias_out, rows_out,
    bias_send, bias_recv, pb_send, pb_recv, y_send, y_recv, core_sems,
):
    me, count = me_and_count(pb_size, ka_size)
    pb, ka = lax.axis_index("pb"), lax.axis_index("ka")
    y_size = ka_size // 2
    y, core = ka // 2, lax.rem(ka, 2)
    greet_all(me, count, ka_size)
    stage_one = []
    for k in range(1, pb_size):
        copy = pltpu.make_async_remote_copy(
            src_ref=rows_ref,
            dst_ref=rows_out.at[core, y, pb],
            send_sem=pb_send.at[k],
            recv_sem=pb_recv.at[k],
            device_id=(lax.rem(pb + k, pb_size), ka),
            device_id_type=MESH,
        )
        copy.start()
        stage_one.append(copy)
    bias_copies = push_all(lambda peer: bias_ref, bias_out, bias_send, bias_recv, me, count, ka_size)
    rows_out[core, y, pb] = rows_ref[...]
    bias_out[me] = bias_ref[...]
    for copy in stage_one:
        copy.wait()
    stage_two = []
    for k in range(1, y_size):
        copy = pltpu.make_async_remote_copy(
            src_ref=rows_out.at[core, y],
            dst_ref=rows_out.at[core, y],
            send_sem=y_send.at[k],
            recv_sem=y_recv.at[k],
            device_id=(pb, lax.rem(y + k, y_size) * 2 + core),
            device_id_type=MESH,
        )
        copy.start()
        stage_two.append(copy)
    for copy in bias_copies:
        copy.wait()
    for copy in stage_two:
        copy.wait()
    copy = pltpu.make_async_remote_copy(
        src_ref=rows_out.at[core],
        dst_ref=rows_out.at[core],
        send_sem=core_sems.at[0],
        recv_sem=core_sems.at[1],
        device_id=(pb, y * 2 + 1 - core),
        device_id_type=MESH,
    )
    copy.start()
    copy.wait()


def entry_gather(bias, rows, pb_size, ka_size):
    count = pb_size * ka_size
    dma = pltpu.SemaphoreType.DMA
    return pl.pallas_call(
        lambda *refs: entry_kernel(pb_size, ka_size, *refs),
        out_shape=(
            jax.ShapeDtypeStruct((count,) + bias.shape, bias.dtype),
            jax.ShapeDtypeStruct((2, ka_size // 2, pb_size) + rows.shape, rows.dtype),
        ),
        in_specs=[VMEM, VMEM],
        out_specs=(VMEM, VMEM),
        scratch_shapes=[
            dma((count,)), dma((count,)), dma((pb_size,)), dma((pb_size,)),
            dma((ka_size,)), dma((ka_size,)), dma((2,)),
        ],
        compiler_params=pltpu.CompilerParams(collective_id=0, has_side_effects=True),
        name="entry_gather",
    )(bias, rows)


def exit_kernel(
    pb_size, ka_size, scale, dq_ref, bias_ref, dq_out, bias_out,
    dq_slots, bias_slots, dq_send, dq_recv, bias_send, bias_recv,
):
    me, count = me_and_count(pb_size, ka_size)
    greet_all(me, count, ka_size)
    copies = push_all(lambda peer: dq_ref.at[peer], dq_slots, dq_send, dq_recv, me, count, ka_size)
    copies += push_all(
        lambda peer: bias_ref.at[peer], bias_slots, bias_send, bias_recv, me, count, ka_size
    )
    dq_slots[me] = dq_ref[me]
    bias_slots[me] = bias_ref[me]
    for copy in copies:
        copy.wait()
    total = dq_slots[0].astype(jnp.float32)
    diag = bias_slots[0]
    for k in range(1, count):
        total = total + dq_slots[k].astype(jnp.float32)
        diag = diag + bias_slots[k]
    dq_out[...] = (total.T * scale).astype(dq_out.dtype)
    bias_out[...] = diag


def exit_reduce(dq, bias, scale, pb_size, ka_size):
    count = pb_size * ka_size
    dma = pltpu.SemaphoreType.DMA
    return pl.pallas_call(
        lambda *refs: exit_kernel(pb_size, ka_size, scale, *refs),
        out_shape=(
            jax.ShapeDtypeStruct((dq.shape[2], dq.shape[1]), jnp.bfloat16),
            jax.ShapeDtypeStruct(bias.shape[1:], jnp.float32),
        ),
        in_specs=[VMEM, VMEM],
        out_specs=(VMEM, VMEM),
        scratch_shapes=[
            pltpu.VMEM(dq.shape, dq.dtype), pltpu.VMEM(bias.shape, bias.dtype),
            dma((count,)), dma((count,)), dma((count,)), dma((count,)),
        ],
        compiler_params=pltpu.CompilerParams(collective_id=2, has_side_effects=True),
        name="exit_reduce",
    )(dq, bias)


def build_table(w_ref, t_ref, tiles):
    def one(t, carry):
        first = w_ref[pl.ds(tiles - 1 - t, 1), :]
        second = w_ref[pl.ds(tiles - t, 1), :]
        wide = jnp.broadcast_to(jnp.concatenate([first, second], axis=1), (LANES, 2 * LANES))
        turned = pltpu.roll(wide, LANES + 1, axis=1, stride=1, stride_axis=0)
        t_ref[pl.ds(pl.multiple_of(t * LANES, LANES), LANES), :] = turned[:, :LANES]
        return carry

    lax.fori_loop(0, tiles, one, 0)


def forward_kernel(
    key_rows, factor, w_ref, q_ref, g_ref, k_ref, v_ref, out_ref, t_ref, m_ref, l_ref, d_ref
):
    step = pl.program_id(0)
    chunk = k_ref.shape[0]
    blocks = q_ref.shape[0] // LANES
    tiles = t_ref.shape[0] // LANES

    @pl.when(step == 0)
    def _():
        build_table(w_ref, t_ref, tiles)
        m_ref[...] = jnp.full_like(m_ref, FLOOR)
        l_ref[...] = jnp.zeros_like(l_ref)
        d_ref[...] = jnp.zeros_like(d_ref)

    def one(kb, carry):
        at = pl.multiple_of(kb * key_rows, key_rows)
        scores = dot_nt(k_ref[pl.ds(at, key_rows), :], q_ref[...])
        dprobs = dot_nt(v_ref[pl.ds(at, key_rows), :], g_ref[...])
        for b in range(blocks):
            lanes = slice(b * LANES, (b + 1) * LANES)
            kappa = pl.multiple_of(step * chunk + at + LANES * (blocks - 1 - b), LANES)
            s = scores[:, lanes] * factor + t_ref[pl.ds(kappa, key_rows), :]
            s = s.reshape(key_rows // 8, 8, LANES)
            d = dprobs[:, lanes].reshape(key_rows // 8, 8, LANES)
            old = m_ref[:, lanes]
            new = jnp.maximum(old, jnp.max(s, axis=0))
            e = jnp.exp2(s - new[None])
            alpha = jnp.exp2(old - new)
            m_ref[:, lanes] = new
            l_ref[:, lanes] = l_ref[:, lanes] * alpha + jnp.sum(e, axis=0)
            d_ref[:, lanes] = d_ref[:, lanes] * alpha + jnp.sum(e * d, axis=0)
        return carry

    lax.fori_loop(0, chunk // key_rows, one, 0)

    @pl.when(step == pl.num_programs(0) - 1)
    def _():
        m = m_ref[...]
        top = jnp.max(m, axis=0, keepdims=True)
        share = jnp.exp2(m - top)
        out_ref[0:1, :] = top
        out_ref[1:2, :] = jnp.sum(l_ref[...] * share, axis=0, keepdims=True)
        out_ref[2:3, :] = jnp.sum(d_ref[...] * share, axis=0, keepdims=True)
        out_ref[3:4, :] = jnp.zeros_like(top)


def forward(window, queries, grads, keys, values, factor):
    rows, dim = queries.shape
    count = keys.shape[0]
    chunk = min(1024, count)
    tiles = count // LANES + rows // LANES - 1
    whole = lambda i: (0, 0)
    return pl.pallas_call(
        lambda *refs: forward_kernel(min(256, chunk), factor, *refs),
        out_shape=jax.ShapeDtypeStruct((4, rows), jnp.float32),
        grid=(count // chunk,),
        in_specs=[
            pl.BlockSpec(window.shape, whole),
            pl.BlockSpec((rows, dim), whole),
            pl.BlockSpec((rows, dim), whole),
            pl.BlockSpec((chunk, dim), lambda i: (i, 0)),
            pl.BlockSpec((chunk, dim), lambda i: (i, 0)),
        ],
        out_specs=pl.BlockSpec((4, rows), whole),
        scratch_shapes=[
            pltpu.VMEM((tiles * LANES, LANES), jnp.float32),
            pltpu.VMEM((8, rows), jnp.float32),
            pltpu.VMEM((8, rows), jnp.float32),
            pltpu.VMEM((8, rows), jnp.float32),
        ],
        name="forward",
    )(window, queries, grads, keys, values)


def fold_diagonals(g_ref, diag_ref, tiles):
    diag_ref[...] = jnp.zeros_like(diag_ref)

    def one(t, carry):
        tile = g_ref[pl.ds(pl.multiple_of(t * LANES, LANES), LANES), :]
        x = jnp.concatenate([tile, jnp.zeros_like(tile)], axis=1)
        half = LANES // 2
        while half >= 8:
            x = pltpu.roll(x[:half], half, axis=1) + x[half:]
            half //= 2
        for part in (4, 2, 1):
            x = pltpu.roll(x, part, axis=1) + pltpu.roll(x, 8 - part, axis=0)
        low = pl.ds(tiles - 1 - t, 1)
        high = pl.ds(tiles - t, 1)
        diag_ref[low, :] = diag_ref[low, :] + x[0:1, :LANES]
        diag_ref[high, :] = diag_ref[high, :] + x[0:1, LANES:]
        return carry

    lax.fori_loop(0, tiles, one, 0)


def backward_kernel(
    key_rows, factor, scale, w_ref, rows_ref, lse_ref, dots_ref, k_ref, v_ref, kt_ref,
    dq_ref, dk_ref, dv_ref, diag_ref, t_ref, g_ref, dk_acc, dv_acc, dq_acc,
):
    step = pl.program_id(0)
    dim = k_ref.shape[1]
    chunk = lse_ref.shape[1]
    blocks = chunk // LANES
    tiles = t_ref.shape[0] // LANES
    last_block = tiles - k_ref.shape[0] // LANES

    @pl.when(step == 0)
    def _():
        build_table(w_ref, t_ref, tiles)
        g_ref[...] = jnp.zeros_like(g_ref)
        dk_acc[...] = jnp.zeros_like(dk_acc)
        dv_acc[...] = jnp.zeros_like(dv_acc)

    rows = rows_ref[...].reshape(chunk, 2 * dim)
    q, g = rows[:, :dim], rows[:, dim:]
    dq_acc[...] = jnp.zeros_like(dq_acc)

    def one(kb, carry):
        at = pl.multiple_of(kb * key_rows, key_rows)
        here = pl.ds(at, key_rows)
        scores = dot_nt(k_ref[here, :], q)
        dprobs = dot_nt(v_ref[here, :], g)
        probs_low, dscores_low = [], []
        for b in range(blocks):
            lanes = slice(b * LANES, (b + 1) * LANES)
            kappa = pl.multiple_of(at + LANES * (last_block - step * blocks - b), LANES)
            there = pl.ds(kappa, key_rows)
            s = scores[:, lanes] * factor + t_ref[there, :]
            p = jnp.exp2(s - lse_ref[:, lanes])
            ds = p * (dprobs[:, lanes] - dots_ref[:, lanes])
            g_ref[there, :] = g_ref[there, :] + ds
            probs_low.append(p.astype(jnp.bfloat16))
            dscores_low.append(ds.astype(jnp.bfloat16))
        p_low = jnp.concatenate(probs_low, axis=1)
        ds_low = jnp.concatenate(dscores_low, axis=1)
        dv_acc[here, :] += dot_nn(p_low, g)
        dk_acc[here, :] += dot_nn(ds_low, q)
        dq_acc[...] += dot_nn(kt_ref[kb], ds_low)
        return carry

    lax.fori_loop(0, k_ref.shape[0] // key_rows, one, 0)

    width = dq_ref.shape[2]
    for b in range(chunk // width):
        dq_ref[b] = dq_acc[:, b * width : (b + 1) * width].astype(dq_ref.dtype)

    @pl.when(step == pl.num_programs(0) - 1)
    def _():
        dk_ref[...] = (dk_acc[...] * scale).astype(dk_ref.dtype)
        dv_ref[...] = dv_acc[...].astype(dv_ref.dtype)
        fold_diagonals(g_ref, diag_ref, tiles)


def backward(window, rows, lse, dots, keys, values, factor, scale):
    parts, steps, part_rows, wide = rows.shape
    count, dim = keys.shape
    chunk = parts * part_rows
    tiles = count // LANES + steps * chunk // LANES - 1
    key_rows = min(256, count)
    keys_turned = keys.reshape(count // key_rows, key_rows, dim).swapaxes(1, 2)
    whole = lambda i: (0, 0)
    f32 = jnp.float32
    return pl.pallas_call(
        lambda *refs: backward_kernel(key_rows, factor, scale, *refs),
        out_shape=(
            jax.ShapeDtypeStruct((parts * steps, dim, part_rows), jnp.bfloat16),
            jax.ShapeDtypeStruct((count, dim), jnp.bfloat16),
            jax.ShapeDtypeStruct((count, dim), jnp.bfloat16),
            jax.ShapeDtypeStruct(window.shape, f32),
        ),
        grid=(steps,),
        in_specs=[
            pl.BlockSpec(window.shape, whole),
            pl.BlockSpec((parts, 1, part_rows, wide), lambda i: (0, i, 0, 0)),
            pl.BlockSpec((1, chunk), lambda i: (0, i)),
            pl.BlockSpec((1, chunk), lambda i: (0, i)),
            pl.BlockSpec((count, dim), whole),
            pl.BlockSpec((count, dim), whole),
            pl.BlockSpec(keys_turned.shape, lambda i: (0, 0, 0)),
        ],
        out_specs=(
            pl.BlockSpec((parts, dim, part_rows), lambda i: (i, 0, 0)),
            pl.BlockSpec((count, dim), whole),
            pl.BlockSpec((count, dim), whole),
            pl.BlockSpec(window.shape, whole),
        ),
        scratch_shapes=[
            pltpu.VMEM((tiles * LANES, LANES), f32),
            pltpu.VMEM((tiles * LANES, LANES), f32),
            pltpu.VMEM((count, dim), f32),
            pltpu.VMEM((count, dim), f32),
            pltpu.VMEM((dim, chunk), f32),
        ],
        name="backward",
    )(window, rows, lse, dots, keys, values, keys_turned)


def on_device(queries, keys, values, bias, grad_out, group_start):
    pb_size, ka_size = lax.axis_size("pb"), lax.axis_size("ka")
    pb, ka = lax.axis_index("pb"), lax.axis_index("ka")
    rows, dim = queries.shape
    key_count = keys.shape[0]
    total_rows = rows * pb_size
    scale = dim ** (-0.5)
    factor = scale * LOG2E
    first = group_start[0]

    part_rows = rows // ka_size
    both = jnp.concatenate([queries, grad_out], axis=1)
    own_rows = lax.dynamic_slice_in_dim(both, ka * part_rows, part_rows, 0)
    bias_all, row_all = entry_gather(bias.reshape(-1, LANES), own_rows, pb_size, ka_size)
    row_all = row_all.swapaxes(0, 1).reshape(ka_size, pb_size, part_rows, 2 * dim)

    bias_count = bias.shape[0] * pb_size * ka_size
    margin = key_count * ka_size
    tail = 2 * LANES
    table = jnp.concatenate(
        [
            jnp.full((margin,), NEGATIVE, jnp.float32),
            bias_all.reshape(-1) * LOG2E,
            jnp.zeros((tail,), jnp.float32),
        ]
    )

    def window_of(query_first, key_first, query_rows, key_rows):
        low = query_first - key_first - key_rows + 1 + margin
        size = key_rows + query_rows
        return low, lax.dynamic_slice_in_dim(table, low, size).reshape(-1, LANES)

    key_base = ka * key_count
    low, window = window_of(first + pb * rows, key_base, rows, key_count)
    stats = forward(window, queries, grad_out, keys, values, factor)
    stats_all = gather_small(stats.reshape(-1, LANES), pb_size, ka_size, 1)
    stats_all = stats_all.reshape(pb_size, ka_size, 4, rows)
    top = jnp.max(stats_all[:, :, 0], axis=1)
    share = jnp.exp2(stats_all[:, :, 0] - top[:, None])
    row_sum = jnp.sum(stats_all[:, :, 1] * share, axis=1)
    lse = (top + jnp.log2(row_sum)).reshape(1, total_rows)
    dots = (jnp.sum(stats_all[:, :, 2] * share, axis=1) / row_sum).reshape(1, total_rows)

    own_count = key_count // pb_size
    own_keys = lax.dynamic_slice_in_dim(keys, pb * own_count, own_count, 0)
    own_values = lax.dynamic_slice_in_dim(values, pb * own_count, own_count, 0)
    low, window = window_of(first, key_base + pb * own_count, total_rows, own_count)
    dq, key_grad, value_grad, diag = backward(
        window, row_all, lse, dots, own_keys, own_values, factor, scale
    )
    spread = lax.dynamic_update_slice_in_dim(
        jnp.zeros(table.shape, jnp.float32), diag.reshape(-1), low, 0
    )
    spread = spread[margin : margin + bias_count].reshape(pb_size * ka_size, -1, LANES)
    query_grad, bias_grad = exit_reduce(dq, spread, scale, pb_size, ka_size)
    return query_grad, key_grad, value_grad, bias_grad.reshape(-1)


def solution(mesh):
    return jax.shard_map(
        on_device,
        mesh=mesh,
        in_specs=(P("pb", None), P("ka", None), P("ka", None), P(("pb", "ka")), P("pb", None), P()),
        out_specs=(
            P(("pb", "ka"), None),
            P(("ka", "pb"), None),
            P(("ka", "pb"), None),
            P(("pb", "ka")),
        ),
        check_vma=False,
    )
```

```python
import math

import jax
import jax.numpy as jnp
from jax import lax
from jax.experimental import pallas as pl
from jax.experimental.pallas import tpu as pltpu
from jax.sharding import PartitionSpec as P

LANES = 128
NEGATIVE = -1e30
FLOOR = -1e20
LOG2E = math.log2(math.e)
MESH = pl.DeviceIdType.MESH
VMEM = pl.BlockSpec(memory_space=pltpu.VMEM)


def dot_nt(a, b):
    return lax.dot_general(a, b, (((1,), (1,)), ((), ())), preferred_element_type=jnp.float32)


def dot_nn(a, b):
    return jnp.dot(a, b, preferred_element_type=jnp.float32)


def signal_peers(peers):
    barrier = pltpu.get_barrier_semaphore()
    for peer in peers:
        pl.semaphore_signal(barrier, inc=1, device_id=peer, device_id_type=MESH)


def await_peers(count):
    pl.semaphore_wait(pltpu.get_barrier_semaphore(), count)


def push(src, dst, send_sem, recv_sem, peer):
    return pltpu.make_async_remote_copy(
        src_ref=src, dst_ref=dst, send_sem=send_sem, recv_sem=recv_sem,
        device_id=peer, device_id_type=MESH,
    )


def pb_peers(pb, ka, pb_size):
    return [(lax.rem(pb + k, pb_size), ka) for k in range(1, pb_size)]


def ka_peers(pb, ka, ka_size):
    return [(pb, lax.rem(ka + k, ka_size)) for k in range(1, ka_size)]


def run_all(copies):
    for copy in copies:
        copy.start()
    return copies


def wait_all(copies):
    for copy in copies:
        copy.wait()


dma = pltpu.SemaphoreType.DMA


def small_call(body, out_shape, scratch, collective_id, name, *operands):
    return pl.pallas_call(
        body,
        out_shape=out_shape,
        in_specs=[VMEM] * len(operands),
        out_specs=VMEM,
        scratch_shapes=scratch,
        compiler_params=pltpu.CompilerParams(collective_id=collective_id, has_side_effects=True),
        name=name,
    )(*operands)


def bias_gather(bias, pb_size, ka_size):
    def body(x_ref, out_ref, pb_send, pb_recv, ka_send, ka_recv):
        pb, ka = lax.axis_index("pb"), lax.axis_index("ka")
        over_pb, over_ka = pb_peers(pb, ka, pb_size), ka_peers(pb, ka, ka_size)
        signal_peers(over_pb + over_ka)
        out_ref[ka, pb] = x_ref[...]
        await_peers(len(over_pb) + len(over_ka))
        wait_all(run_all([
            push(x_ref, out_ref.at[ka, pb], pb_send.at[k], pb_recv.at[k], peer)
            for k, peer in enumerate(over_pb)
        ]))
        wait_all(run_all([
            push(out_ref.at[ka], out_ref.at[ka], ka_send.at[k], ka_recv.at[k], peer)
            for k, peer in enumerate(over_ka)
        ]))

    return small_call(
        body,
        jax.ShapeDtypeStruct((ka_size, pb_size) + bias.shape, bias.dtype),
        [dma((pb_size,)), dma((pb_size,)), dma((ka_size,)), dma((ka_size,))],
        0, "bias_gather", bias,
    )


def stats_exchange(stats, pb_size, ka_size):
    def body(x_ref, out_ref, slots, own, pb_send, pb_recv, ka_send, ka_recv):
        pb, ka = lax.axis_index("pb"), lax.axis_index("ka")
        over_pb, over_ka = pb_peers(pb, ka, pb_size), ka_peers(pb, ka, ka_size)
        signal_peers(over_pb + over_ka)
        slots[ka] = x_ref[...]
        await_peers(len(over_pb) + len(over_ka))
        wait_all(run_all([
            push(x_ref, slots.at[ka], ka_send.at[k], ka_recv.at[k], peer)
            for k, peer in enumerate(over_ka)
        ]))
        top = slots[0, 0:1, :]
        for k in range(1, ka_size):
            top = jnp.maximum(top, slots[k, 0:1, :])
        row_sum, dots = jnp.zeros_like(top), jnp.zeros_like(top)
        for k in range(ka_size):
            share = jnp.exp2(slots[k, 0:1, :] - top)
            row_sum = row_sum + slots[k, 1:2, :] * share
            dots = dots + slots[k, 2:3, :] * share
        joined = jnp.concatenate([top + jnp.log2(row_sum), dots / row_sum], axis=0)
        own[...] = joined
        out_ref[pb] = joined
        wait_all(run_all([
            push(own, out_ref.at[pb], pb_send.at[k], pb_recv.at[k], peer)
            for k, peer in enumerate(over_pb)
        ]))

    rows = stats.shape[1]
    return small_call(
        body,
        jax.ShapeDtypeStruct((pb_size, 2, rows), jnp.float32),
        [
            pltpu.VMEM((ka_size,) + stats.shape, jnp.float32),
            pltpu.VMEM((2, rows), jnp.float32),
            dma((pb_size,)), dma((pb_size,)), dma((ka_size,)), dma((ka_size,)),
        ],
        1, "stats_exchange", stats,
    )


def diagonal_reduce(spread):
    pb_size, ka_size = spread.shape[:2]

    def body(x_ref, out_ref, slots, part, got, pb_send, pb_recv, ka_send, ka_recv):
        pb, ka = lax.axis_index("pb"), lax.axis_index("ka")
        over_pb, over_ka = pb_peers(pb, ka, pb_size), ka_peers(pb, ka, ka_size)
        signal_peers(over_pb + over_ka)
        slots[ka] = x_ref[:, ka]
        await_peers(len(over_pb) + len(over_ka))
        wait_all(run_all([
            push(x_ref.at[:, peer[1]], slots.at[ka], ka_send.at[k], ka_recv.at[k], peer)
            for k, peer in enumerate(over_ka)
        ]))
        total = slots[0]
        for k in range(1, ka_size):
            total = total + slots[k]
        part[...] = total
        got[pb] = part[pb]
        wait_all(run_all([
            push(part.at[peer[0]], got.at[pb], pb_send.at[k], pb_recv.at[k], peer)
            for k, peer in enumerate(over_pb)
        ]))
        total = got[0]
        for k in range(1, pb_size):
            total = total + got[k]
        out_ref[...] = total

    block = spread.shape[2:]
    f32 = jnp.float32
    return small_call(
        body,
        jax.ShapeDtypeStruct(block, f32),
        [
            pltpu.VMEM((ka_size, pb_size) + block, f32),
            pltpu.VMEM((pb_size,) + block, f32),
            pltpu.VMEM((pb_size,) + block, f32),
            dma((pb_size,)), dma((pb_size,)), dma((ka_size,)), dma((ka_size,)),
        ],
        2, "diagonal_reduce", spread,
    )


def build_table(w_ref, t_ref, tiles):
    def one(t, carry):
        first = w_ref[pl.ds(tiles - 1 - t, 1), :]
        second = w_ref[pl.ds(tiles - t, 1), :]
        wide = jnp.broadcast_to(jnp.concatenate([first, second], axis=1), (LANES, 2 * LANES))
        turned = pltpu.roll(wide, LANES + 1, axis=1, stride=1, stride_axis=0)
        t_ref[pl.ds(pl.multiple_of(t * LANES, LANES), LANES), :] = turned[:, :LANES]
        return carry

    lax.fori_loop(0, tiles, one, 0)


def stage_of(k, steps, pb_size):
    return 0 if k == 0 else 1 + (k - 1) * (steps - 1) // max(pb_size - 1, 1)


def forward_kernel(
    key_rows, factor, steps, pb_size, ka_size,
    w_ref, q_ref, g_ref, k_ref, v_ref, rows_ref, out_ref, rows_out,
    t_ref, m_ref, l_ref, d_ref,
    own_sem, pb_send, pb_recv, y_send, y_recv, core_send, core_recv,
):
    step = pl.program_id(0)
    chunk = k_ref.shape[0]
    blocks = q_ref.shape[0] // LANES
    tiles = t_ref.shape[0] // LANES
    pb, ka = lax.axis_index("pb"), lax.axis_index("ka")
    y_size = ka_size // 2
    y, core = ka // 2, lax.rem(ka, 2)
    over_pb = pb_peers(pb, ka, pb_size)
    over_y = [(pb, lax.rem(y + j, y_size) * 2 + core) for j in range(1, y_size)]
    partner = (pb, y * 2 + 1 - core)
    peers = over_pb + over_y + [partner]

    own_copy = pltpu.make_async_copy(rows_ref, rows_out.at[core, y, pb], own_sem)
    pb_copies = [
        push(rows_ref, rows_out.at[core, y, pb], pb_send.at[k], pb_recv.at[k], peer)
        for k, peer in enumerate(over_pb)
    ]

    def slot_of(k):
        return lax.rem(pb + pb_size - k, pb_size)

    def y_copies(k):
        slot = slot_of(k)
        source = rows_ref if k == 0 else rows_out.at[core, y, slot]
        return [
            push(source, rows_out.at[core, y, slot], y_send.at[j, k], y_recv.at[j, k], peer)
            for j, peer in enumerate(over_y)
        ]

    def core_copy(k):
        here = rows_out.at[core, :, slot_of(k)]
        return push(here, here, core_send.at[k], core_recv.at[k], partner)

    def relay(k):
        if k == 0:
            own_copy.wait()
        for copy in y_copies(k):
            copy.wait_recv()
        core_copy(k).start()

    @pl.when(step == 0)
    def _():
        signal_peers(peers)
        own_copy.start()
        build_table(w_ref, t_ref, tiles)
        m_ref[...] = jnp.full_like(m_ref, FLOOR)
        l_ref[...] = jnp.zeros_like(l_ref)
        d_ref[...] = jnp.zeros_like(d_ref)
        await_peers(len(peers))
        run_all(pb_copies)
        run_all(y_copies(0))

    for s in range(1, steps):
        @pl.when(step == s)
        def _(s=s):
            for k in range(1, pb_size):
                if stage_of(k, steps, pb_size) == s:
                    pb_copies[k - 1].wait_recv()
                    run_all(y_copies(k))
            for k in range(pb_size):
                if stage_of(k, steps, pb_size) == s - 1:
                    relay(k)

    def one(kb, carry):
        at = pl.multiple_of(kb * key_rows, key_rows)
        scores = dot_nt(k_ref[pl.ds(at, key_rows), :], q_ref[...])
        dprobs = dot_nt(v_ref[pl.ds(at, key_rows), :], g_ref[...])
        for b in range(blocks):
            lanes = slice(b * LANES, (b + 1) * LANES)
            kappa = pl.multiple_of(step * chunk + at + LANES * (blocks - 1 - b), LANES)
            s = scores[:, lanes] * factor + t_ref[pl.ds(kappa, key_rows), :]
            s = s.reshape(key_rows // 8, 8, LANES)
            d = dprobs[:, lanes].reshape(key_rows // 8, 8, LANES)
            old = m_ref[:, lanes]
            new = jnp.maximum(old, jnp.max(s, axis=0))
            e = jnp.exp2(s - new[None])
            alpha = jnp.exp2(old - new)
            m_ref[:, lanes] = new
            l_ref[:, lanes] = l_ref[:, lanes] * alpha + jnp.sum(e, axis=0)
            d_ref[:, lanes] = d_ref[:, lanes] * alpha + jnp.sum(e * d, axis=0)
        return carry

    lax.fori_loop(0, chunk // key_rows, one, 0)

    @pl.when(step == pl.num_programs(0) - 1)
    def _():
        m = m_ref[...]
        top = jnp.max(m, axis=0, keepdims=True)
        share = jnp.exp2(m - top)
        out_ref[0:1, :] = top
        out_ref[1:2, :] = jnp.sum(l_ref[...] * share, axis=0, keepdims=True)
        out_ref[2:3, :] = jnp.sum(d_ref[...] * share, axis=0, keepdims=True)
        out_ref[3:4, :] = jnp.zeros_like(top)
        for k in range(pb_size):
            if stage_of(k, steps, pb_size) == steps - 1:
                relay(k)
        for copy in pb_copies:
            copy.wait_send()
        for k in range(pb_size):
            for copy in y_copies(k):
                copy.wait_send()
            core_copy(k).wait()


def forward(window, queries, grads, keys, values, own_rows, factor, pb_size, ka_size):
    rows, dim = queries.shape
    count = keys.shape[0]
    chunk = min(1024, count // 4)
    tiles = count // LANES + rows // LANES - 1
    whole = lambda i: (0, 0)
    return pl.pallas_call(
        lambda *refs: forward_kernel(
            min(256, chunk), factor, count // chunk, pb_size, ka_size, *refs
        ),
        out_shape=(
            jax.ShapeDtypeStruct((4, rows), jnp.float32),
            jax.ShapeDtypeStruct((2, ka_size // 2, pb_size) + own_rows.shape, own_rows.dtype),
        ),
        grid=(count // chunk,),
        in_specs=[
            pl.BlockSpec(window.shape, whole),
            pl.BlockSpec((rows, dim), whole),
            pl.BlockSpec((rows, dim), whole),
            pl.BlockSpec((chunk, dim), lambda i: (i, 0)),
            pl.BlockSpec((chunk, dim), lambda i: (i, 0)),
            pl.BlockSpec(memory_space=pl.ANY),
        ],
        out_specs=(pl.BlockSpec((4, rows), whole), pl.BlockSpec(memory_space=pl.ANY)),
        scratch_shapes=[
            pltpu.VMEM((tiles * LANES, LANES), jnp.float32),
            pltpu.VMEM((8, rows), jnp.float32),
            pltpu.VMEM((8, rows), jnp.float32),
            pltpu.VMEM((8, rows), jnp.float32),
            dma, dma((pb_size,)), dma((pb_size,)), dma((ka_size, pb_size)), dma((ka_size, pb_size)),
            dma((pb_size,)), dma((pb_size,)),
        ],
        compiler_params=pltpu.CompilerParams(collective_id=3, has_side_effects=True),
        name="forward",
    )(window, queries, grads, keys, values, own_rows)


def fold_diagonals(g_ref, diag_ref, tiles):
    diag_ref[...] = jnp.zeros_like(diag_ref)

    def one(t, carry):
        tile = g_ref[pl.ds(pl.multiple_of(t * LANES, LANES), LANES), :]
        x = jnp.concatenate([tile, jnp.zeros_like(tile)], axis=1)
        half = LANES // 2
        while half >= 8:
            x = pltpu.roll(x[:half], half, axis=1) + x[half:]
            half //= 2
        for part in (4, 2, 1):
            x = pltpu.roll(x, part, axis=1) + pltpu.roll(x, 8 - part, axis=0)
        low = pl.ds(tiles - 1 - t, 1)
        high = pl.ds(tiles - t, 1)
        diag_ref[low, :] = diag_ref[low, :] + x[0:1, :LANES]
        diag_ref[high, :] = diag_ref[high, :] + x[0:1, LANES:]
        return carry

    lax.fori_loop(0, tiles, one, 0)


def backward_kernel(
    key_rows, factor, scale, pb_size, ka_size,
    w_ref, rows_ref, stats_ref, k_ref, v_ref, kt_ref,
    dq_ref, dk_ref, dv_ref, diag_ref, t_ref, g_ref, dk_acc, dv_acc, dq_acc,
    dq_sent, dq_got, send_sems, recv_sems,
):
    step = pl.program_id(0)
    dim = k_ref.shape[1]
    chunk = stats_ref.shape[2]
    pb, ka = lax.axis_index("pb"), lax.axis_index("ka")
    turn = lax.rem(pb + 1 + step, pb_size)
    peers = []
    for i in range(pb_size):
        for j in range(ka_size):
            if (i, j) != (pb_size - 1, 0):
                peers.append((lax.rem(pb + 1 + i, pb_size), lax.rem(ka + j, ka_size)))
    here_id = pb * ka_size + ka

    def term_copy(i, j):
        target = lax.rem(ka + j, ka_size)
        return push(
            dq_sent.at[i, target], dq_got.at[here_id], send_sems.at[i, j], recv_sems.at[i, j],
            (lax.rem(pb + 1 + i, pb_size), target),
        )

    blocks = chunk // LANES
    tiles = t_ref.shape[0] // LANES
    last_block = tiles - k_ref.shape[0] // LANES

    @pl.when(step == 0)
    def _():
        signal_peers(peers)
        build_table(w_ref, t_ref, tiles)
        g_ref[...] = jnp.zeros_like(g_ref)
        dk_acc[...] = jnp.zeros_like(dk_acc)
        dv_acc[...] = jnp.zeros_like(dv_acc)

    @pl.when(step == 1)
    def _():
        await_peers(len(peers))

    @pl.when(step >= 1)
    def _():
        for j in range(ka_size):
            term_copy(step - 1, j).start()

    rows = jnp.concatenate([rows_ref[k % 2, k // 2, 0] for k in range(ka_size)], axis=0)
    lse_row, dots_row = stats_ref[0, 0:1, :], stats_ref[0, 1:2, :]
    q, g = rows[:, :dim], rows[:, dim:]
    dq_acc[...] = jnp.zeros_like(dq_acc)

    def one(kb, carry):
        at = pl.multiple_of(kb * key_rows, key_rows)
        here = pl.ds(at, key_rows)
        scores = dot_nt(k_ref[here, :], q)
        dprobs = dot_nt(v_ref[here, :], g)
        probs_low, dscores_low = [], []
        for b in range(blocks):
            lanes = slice(b * LANES, (b + 1) * LANES)
            kappa = pl.multiple_of(at + LANES * (last_block - turn * blocks - b), LANES)
            there = pl.ds(kappa, key_rows)
            s = scores[:, lanes] * factor + t_ref[there, :]
            p = jnp.exp2(s - lse_row[:, lanes])
            ds = p * (dprobs[:, lanes] - dots_row[:, lanes])
            g_ref[there, :] = g_ref[there, :] + ds
            probs_low.append(p.astype(jnp.bfloat16))
            dscores_low.append(ds.astype(jnp.bfloat16))
        p_low = jnp.concatenate(probs_low, axis=1)
        ds_low = jnp.concatenate(dscores_low, axis=1)
        dv_acc[here, :] += dot_nn(p_low, g)
        dk_acc[here, :] += dot_nn(ds_low, q)
        dq_acc[...] += dot_nn(kt_ref[kb], ds_low)
        return carry

    lax.fori_loop(0, k_ref.shape[0] // key_rows, one, 0)

    width = dq_sent.shape[3]
    for b in range(ka_size):
        dq_sent[step, b] = dq_acc[:, b * width : (b + 1) * width].astype(dq_sent.dtype)

    @pl.when(step == pb_size - 1)
    def _():
        dk_ref[...] = (dk_acc[...] * scale).astype(dk_ref.dtype)
        dv_ref[...] = dv_acc[...].astype(dv_ref.dtype)
        for j in range(1, ka_size):
            term_copy(pb_size - 1, j).start()
        dq_got[here_id] = dq_sent[pb_size - 1, ka]
        fold_diagonals(g_ref, diag_ref, tiles)
        for i in range(pb_size):
            for j in range(ka_size):
                if (i, j) != (pb_size - 1, 0):
                    term_copy(i, j).wait()
        total = dq_got[0].astype(jnp.float32)
        for k in range(1, pb_size * ka_size):
            total = total + dq_got[k].astype(jnp.float32)
        dq_ref[...] = (total.T * scale).astype(dq_ref.dtype)


def backward(window, rows, stats, keys, values, factor, scale):
    cores, y_size, pb_size, part_rows, wide = rows.shape
    ka_size = cores * y_size
    count, dim = keys.shape
    chunk = ka_size * part_rows
    tiles = count // LANES + pb_size * chunk // LANES - 1
    key_rows = min(256, count)
    keys_turned = keys.reshape(count // key_rows, key_rows, dim).swapaxes(1, 2)
    whole = lambda i: (0, 0)
    f32 = jnp.float32

    def turn(i):
        return lax.rem(lax.axis_index("pb") + 1 + i, pb_size)

    return pl.pallas_call(
        lambda *refs: backward_kernel(key_rows, factor, scale, pb_size, ka_size, *refs),
        out_shape=(
            jax.ShapeDtypeStruct((part_rows, dim), jnp.bfloat16),
            jax.ShapeDtypeStruct((count, dim), jnp.bfloat16),
            jax.ShapeDtypeStruct((count, dim), jnp.bfloat16),
            jax.ShapeDtypeStruct(window.shape, f32),
        ),
        grid=(pb_size,),
        in_specs=[
            pl.BlockSpec(window.shape, whole),
            pl.BlockSpec((cores, y_size, 1, part_rows, wide), lambda i: (0, 0, turn(i), 0, 0)),
            pl.BlockSpec((1, 2, chunk), lambda i: (turn(i), 0, 0)),
            pl.BlockSpec((count, dim), whole),
            pl.BlockSpec((count, dim), whole),
            pl.BlockSpec(keys_turned.shape, lambda i: (0, 0, 0)),
        ],
        out_specs=(
            pl.BlockSpec((part_rows, dim), whole),
            pl.BlockSpec((count, dim), whole),
            pl.BlockSpec((count, dim), whole),
            pl.BlockSpec(window.shape, whole),
        ),
        scratch_shapes=[
            pltpu.VMEM((tiles * LANES, LANES), f32),
            pltpu.VMEM((tiles * LANES, LANES), f32),
            pltpu.VMEM((count, dim), f32),
            pltpu.VMEM((count, dim), f32),
            pltpu.VMEM((dim, chunk), f32),
            pltpu.VMEM((pb_size, ka_size, dim, part_rows), jnp.bfloat16),
            pltpu.VMEM((pb_size * ka_size, dim, part_rows), jnp.bfloat16),
            dma((pb_size, ka_size)), dma((pb_size, ka_size)),
        ],
        compiler_params=pltpu.CompilerParams(collective_id=4, has_side_effects=True),
        name="backward",
    )(window, rows, stats, keys, values, keys_turned)


def on_device(queries, keys, values, bias, grad_out, group_start):
    pb_size, ka_size = lax.axis_size("pb"), lax.axis_size("ka")
    pb, ka = lax.axis_index("pb"), lax.axis_index("ka")
    rows, dim = queries.shape
    key_count = keys.shape[0]
    total_rows = rows * pb_size
    scale = dim ** (-0.5)
    factor = scale * LOG2E
    first = group_start[0]

    part_rows = rows // ka_size
    both = jnp.concatenate([queries, grad_out], axis=1)
    own_rows = lax.dynamic_slice_in_dim(both, ka * part_rows, part_rows, 0)
    bias_all = bias_gather(bias.reshape(-1, LANES), pb_size, ka_size).swapaxes(0, 1)

    bias_count = bias.shape[0] * pb_size * ka_size
    margin = key_count * ka_size
    tail = 2 * LANES
    table = jnp.concatenate(
        [
            jnp.full((margin,), NEGATIVE, jnp.float32),
            bias_all.reshape(-1) * LOG2E,
            jnp.zeros((tail,), jnp.float32),
        ]
    )

    def window_of(query_first, key_first, query_rows, key_rows):
        low = query_first - key_first - key_rows + 1 + margin
        size = key_rows + query_rows
        return low, lax.dynamic_slice_in_dim(table, low, size).reshape(-1, LANES)

    key_base = ka * key_count
    low, window = window_of(first + pb * rows, key_base, rows, key_count)
    stats, row_all = forward(
        window, queries, grad_out, keys, values, own_rows, factor, pb_size, ka_size
    )
    stats = stats_exchange(stats, pb_size, ka_size)

    own_count = key_count // pb_size
    own_keys = lax.dynamic_slice_in_dim(keys, pb * own_count, own_count, 0)
    own_values = lax.dynamic_slice_in_dim(values, pb * own_count, own_count, 0)
    low, window = window_of(first, key_base + pb * own_count, total_rows, own_count)
    query_grad, key_grad, value_grad, diag = backward(
        window, row_all, stats, own_keys, own_values, factor, scale
    )
    spread = lax.dynamic_update_slice_in_dim(
        jnp.zeros(table.shape, jnp.float32), diag.reshape(-1), low, 0
    )
    spread = spread[margin : margin + bias_count].reshape(pb_size, ka_size, -1, LANES)
    bias_grad = diagonal_reduce(spread)
    return query_grad, key_grad, value_grad, bias_grad.reshape(-1)


def solution(mesh):
    return jax.shard_map(
        on_device,
        mesh=mesh,
        in_specs=(P("pb", None), P("ka", None), P("ka", None), P(("pb", "ka")), P("pb", None), P()),
        out_specs=(
            P(("pb", "ka"), None),
            P(("ka", "pb"), None),
            P(("ka", "pb"), None),
            P(("pb", "ka")),
        ),
        check_vma=False,
    )
```

```python
import math

import jax
import jax.numpy as jnp
from jax import lax
from jax.experimental import pallas as pl
from jax.experimental.pallas import tpu as pltpu
from jax.sharding import PartitionSpec as P

LANES = 128
NEGATIVE = -1e30
FLOOR = -1e20
LOG2E = math.log2(math.e)
MESH = pl.DeviceIdType.MESH
VMEM = pl.BlockSpec(memory_space=pltpu.VMEM)


def dot_nt(a, b):
    return lax.dot_general(a, b, (((1,), (1,)), ((), ())), preferred_element_type=jnp.float32)


def dot_nn(a, b):
    return jnp.dot(a, b, preferred_element_type=jnp.float32)


def signal_peers(peers):
    barrier = pltpu.get_barrier_semaphore()
    for peer in peers:
        pl.semaphore_signal(barrier, inc=1, device_id=peer, device_id_type=MESH)


def await_peers(count):
    pl.semaphore_wait(pltpu.get_barrier_semaphore(), count)


def push(src, dst, send_sem, recv_sem, peer):
    return pltpu.make_async_remote_copy(
        src_ref=src, dst_ref=dst, send_sem=send_sem, recv_sem=recv_sem,
        device_id=peer, device_id_type=MESH,
    )


def pb_peers(pb, ka, pb_size):
    return [(lax.rem(pb + k, pb_size), ka) for k in range(1, pb_size)]


def ka_peers(pb, ka, ka_size):
    return [(pb, lax.rem(ka + k, ka_size)) for k in range(1, ka_size)]


def run_all(copies):
    for copy in copies:
        copy.start()
    return copies


def wait_all(copies):
    for copy in copies:
        copy.wait()


dma = pltpu.SemaphoreType.DMA


def small_call(body, out_shape, scratch, collective_id, name, *operands):
    return pl.pallas_call(
        body,
        out_shape=out_shape,
        in_specs=[VMEM] * len(operands),
        out_specs=jax.tree.map(lambda leaf: VMEM, out_shape),
        scratch_shapes=scratch,
        compiler_params=pltpu.CompilerParams(collective_id=collective_id, has_side_effects=True),
        name=name,
    )(*operands)


def entry_gather(bias, rows, pb_size, ka_size):
    def body(
        x_ref, rows_ref, out_ref, rows_out,
        pb_send, pb_recv, ka_send, ka_recv, rows_send, rows_recv,
    ):
        pb, ka = lax.axis_index("pb"), lax.axis_index("ka")
        over_pb, over_ka = pb_peers(pb, ka, pb_size), ka_peers(pb, ka, ka_size)
        signal_peers(over_pb + over_ka)
        out_ref[ka, pb] = x_ref[...]
        await_peers(len(over_pb) + len(over_ka))
        first = run_all([
            push(x_ref, out_ref.at[ka, pb], pb_send.at[k], pb_recv.at[k], peer)
            for k, peer in enumerate(over_pb)
        ])
        rows_copies = run_all([
            push(rows_ref, rows_out.at[pb], rows_send.at[k], rows_recv.at[k], peer)
            for k, peer in enumerate(over_pb)
        ])
        rows_out[pb] = rows_ref[...]
        wait_all(first)
        wait_all(run_all([
            push(out_ref.at[ka], out_ref.at[ka], ka_send.at[k], ka_recv.at[k], peer)
            for k, peer in enumerate(over_ka)
        ]))
        wait_all(rows_copies)

    return small_call(
        body,
        (
            jax.ShapeDtypeStruct((ka_size, pb_size) + bias.shape, bias.dtype),
            jax.ShapeDtypeStruct((pb_size,) + rows.shape, rows.dtype),
        ),
        [dma((pb_size,)), dma((pb_size,)), dma((ka_size,)), dma((ka_size,)),
         dma((pb_size,)), dma((pb_size,))],
        0, "entry_gather", bias, rows,
    )


def diagonal_reduce(spread):
    pb_size, ka_size = spread.shape[:2]

    def body(x_ref, out_ref, slots, part, got, pb_send, pb_recv, ka_send, ka_recv):
        pb, ka = lax.axis_index("pb"), lax.axis_index("ka")
        over_pb, over_ka = pb_peers(pb, ka, pb_size), ka_peers(pb, ka, ka_size)
        signal_peers(over_pb + over_ka)
        slots[ka] = x_ref[:, ka]
        await_peers(len(over_pb) + len(over_ka))
        wait_all(run_all([
            push(x_ref.at[:, peer[1]], slots.at[ka], ka_send.at[k], ka_recv.at[k], peer)
            for k, peer in enumerate(over_ka)
        ]))
        total = slots[0]
        for k in range(1, ka_size):
            total = total + slots[k]
        part[...] = total
        got[pb] = part[pb]
        wait_all(run_all([
            push(part.at[peer[0]], got.at[pb], pb_send.at[k], pb_recv.at[k], peer)
            for k, peer in enumerate(over_pb)
        ]))
        total = got[0]
        for k in range(1, pb_size):
            total = total + got[k]
        out_ref[...] = total

    block = spread.shape[2:]
    f32 = jnp.float32
    return small_call(
        body,
        jax.ShapeDtypeStruct(block, f32),
        [
            pltpu.VMEM((ka_size, pb_size) + block, f32),
            pltpu.VMEM((pb_size,) + block, f32),
            pltpu.VMEM((pb_size,) + block, f32),
            dma((pb_size,)), dma((pb_size,)), dma((ka_size,)), dma((ka_size,)),
        ],
        2, "diagonal_reduce", spread,
    )


def build_table(w_ref, t_ref, tiles):
    def one(t, carry):
        first = w_ref[pl.ds(tiles - 1 - t, 1), :]
        second = w_ref[pl.ds(tiles - t, 1), :]
        wide = jnp.broadcast_to(jnp.concatenate([first, second], axis=1), (LANES, 2 * LANES))
        turned = pltpu.roll(wide, LANES + 1, axis=1, stride=1, stride_axis=0)
        t_ref[pl.ds(pl.multiple_of(t * LANES, LANES), LANES), :] = turned[:, :LANES]
        return carry

    lax.fori_loop(0, tiles, one, 0)


def forward_kernel(
    key_rows, factor, steps, pb_size, ka_size,
    w_ref, q_ref, g_ref, k_ref, v_ref, rows_ref, out_ref, rows_out,
    t_ref, m_ref, l_ref, d_ref,
    slots, joined, own_sem, y_send, y_recv, core_send, core_recv, ka_send, ka_recv, pb_send, pb_recv,
):
    step = pl.program_id(0)
    chunk = k_ref.shape[0]
    blocks = q_ref.shape[0] // LANES
    tiles = t_ref.shape[0] // LANES
    pb, ka = lax.axis_index("pb"), lax.axis_index("ka")
    y_size = ka_size // 2
    y, core = ka // 2, lax.rem(ka, 2)
    over_pb = pb_peers(pb, ka, pb_size)
    over_y = [(pb, lax.rem(y + j, y_size) * 2 + core) for j in range(1, y_size)]
    partner = (pb, y * 2 + 1 - core)
    over_ka = ka_peers(pb, ka, ka_size)
    peers = over_pb + over_ka

    own_copy = pltpu.make_async_copy(rows_ref, rows_out.at[core, y], own_sem)
    y_copies = [
        push(rows_ref, rows_out.at[core, y], y_send.at[j], y_recv.at[j], peer)
        for j, peer in enumerate(over_y)
    ]

    def core_copy(j):
        source = rows_out.at[core, lax.rem(y + y_size - j, y_size)]
        return push(
            rows_ref if j == 0 else source, source, core_send.at[j], core_recv.at[j], partner
        )

    @pl.when(step == 0)
    def _():
        signal_peers(peers)
        own_copy.start()
        build_table(w_ref, t_ref, tiles)
        m_ref[...] = jnp.full_like(m_ref, FLOOR)
        l_ref[...] = jnp.zeros_like(l_ref)
        d_ref[...] = jnp.zeros_like(d_ref)
        await_peers(len(peers))
        run_all(y_copies)
        core_copy(0).start()

    @pl.when(step == steps * 3 // 4)
    def _():
        for j, copy in enumerate(y_copies):
            copy.wait_recv()
            core_copy(j + 1).start()

    def one(kb, carry):
        at = kb * key_rows
        scores = dot_nt(k_ref[pl.ds(at, key_rows), :], q_ref[...])
        dprobs = dot_nt(v_ref[pl.ds(at, key_rows), :], g_ref[...])
        for b in range(blocks):
            lanes = slice(b * LANES, (b + 1) * LANES)
            kappa = pl.multiple_of(step * chunk + at + LANES * (blocks - 1 - b), LANES)
            s = scores[:, lanes] * factor + t_ref[pl.ds(kappa, key_rows), :]
            s = s.reshape(key_rows // 8, 8, LANES)
            d = dprobs[:, lanes].reshape(key_rows // 8, 8, LANES)
            old = m_ref[:, lanes]
            new = jnp.maximum(old, jnp.max(s, axis=0))
            e = jnp.exp2(s - new[None])
            alpha = jnp.exp2(old - new)
            m_ref[:, lanes] = new
            l_ref[:, lanes] = l_ref[:, lanes] * alpha + jnp.sum(e, axis=0)
            d_ref[:, lanes] = d_ref[:, lanes] * alpha + jnp.sum(e * d, axis=0)
        return carry

    for kb in range(chunk // key_rows):
        one(kb, 0)

    @pl.when(step == pl.num_programs(0) - 1)
    def _():
        m = m_ref[...]
        top = jnp.max(m, axis=0, keepdims=True)
        share = jnp.exp2(m - top)
        slots[ka, 0:1, :] = top
        slots[ka, 1:2, :] = jnp.sum(l_ref[...] * share, axis=0, keepdims=True)
        slots[ka, 2:3, :] = jnp.sum(d_ref[...] * share, axis=0, keepdims=True)
        slots[ka, 3:4, :] = jnp.zeros_like(top)
        stat_copies = run_all([
            push(slots.at[ka], slots.at[ka], ka_send.at[k], ka_recv.at[k], peer)
            for k, peer in enumerate(over_ka)
        ])
        own_copy.wait()
        for copy in y_copies:
            copy.wait_send()
        for j in range(y_size):
            core_copy(j).wait()
        wait_all(stat_copies)
        best = slots[0, 0:1, :]
        for k in range(1, ka_size):
            best = jnp.maximum(best, slots[k, 0:1, :])
        row_sum, dots = jnp.zeros_like(best), jnp.zeros_like(best)
        for k in range(ka_size):
            weight = jnp.exp2(slots[k, 0:1, :] - best)
            row_sum = row_sum + slots[k, 1:2, :] * weight
            dots = dots + slots[k, 2:3, :] * weight
        joined[pb] = jnp.concatenate([best + jnp.log2(row_sum), dots / row_sum], axis=0)
        wait_all(run_all([
            push(joined.at[pb], joined.at[pb], pb_send.at[k], pb_recv.at[k], peer)
            for k, peer in enumerate(over_pb)
        ]))
        out_ref[...] = joined[...]


def forward(window, queries, grads, keys, values, own_rows, factor, pb_size, ka_size):
    rows, dim = queries.shape
    count = keys.shape[0]
    chunk = min(1024, count // 4)
    tiles = count // LANES + rows // LANES - 1
    whole = lambda i: (0, 0)
    return pl.pallas_call(
        lambda *refs: forward_kernel(
            min(256, chunk), factor, count // chunk, pb_size, ka_size, *refs
        ),
        out_shape=(
            jax.ShapeDtypeStruct((pb_size, 2, rows), jnp.float32),
            jax.ShapeDtypeStruct((2, ka_size // 2) + own_rows.shape, own_rows.dtype),
        ),
        grid=(count // chunk,),
        in_specs=[
            pl.BlockSpec(window.shape, whole),
            pl.BlockSpec((rows, dim), whole),
            pl.BlockSpec((rows, dim), whole),
            pl.BlockSpec((chunk, dim), lambda i: (i, 0)),
            pl.BlockSpec((chunk, dim), lambda i: (i, 0)),
            VMEM,
        ],
        out_specs=(VMEM, pl.BlockSpec(memory_space=pl.ANY)),
        scratch_shapes=[
            pltpu.VMEM((tiles * LANES, LANES), jnp.float32),
            pltpu.VMEM((8, rows), jnp.float32),
            pltpu.VMEM((8, rows), jnp.float32),
            pltpu.VMEM((8, rows), jnp.float32),
            pltpu.VMEM((ka_size, 4, rows), jnp.float32),
            pltpu.VMEM((pb_size, 2, rows), jnp.float32),
            dma, dma((ka_size,)), dma((ka_size,)), dma((ka_size,)), dma((ka_size,)),
            dma((ka_size,)), dma((ka_size,)), dma((pb_size,)), dma((pb_size,)),
        ],
        compiler_params=pltpu.CompilerParams(collective_id=3, has_side_effects=True),
        name="forward",
    )(window, queries, grads, keys, values, own_rows)


def fold_diagonals(g_ref, diag_ref, tiles):
    diag_ref[...] = jnp.zeros_like(diag_ref)

    def one(t, carry):
        tile = g_ref[pl.ds(pl.multiple_of(t * LANES, LANES), LANES), :]
        x = jnp.concatenate([tile, jnp.zeros_like(tile)], axis=1)
        half = LANES // 2
        while half >= 8:
            x = pltpu.roll(x[:half], half, axis=1) + x[half:]
            half //= 2
        for part in (4, 2, 1):
            x = pltpu.roll(x, part, axis=1) + pltpu.roll(x, 8 - part, axis=0)
        low = pl.ds(tiles - 1 - t, 1)
        high = pl.ds(tiles - t, 1)
        diag_ref[low, :] = diag_ref[low, :] + x[0:1, :LANES]
        diag_ref[high, :] = diag_ref[high, :] + x[0:1, LANES:]
        return carry

    lax.fori_loop(0, tiles, one, 0)


def backward_kernel(
    key_rows, factor, scale, pb_size, ka_size,
    w_ref, rows_ref, stats_ref, k_ref, v_ref,
    dq_ref, dk_ref, dv_ref, diag_ref, t_ref, g_ref, dk_acc, dv_acc, dq_acc,
    dq_sent, dq_got, kt_ref, send_sems, recv_sems,
):
    step = pl.program_id(0)
    dim = k_ref.shape[1]
    chunk = stats_ref.shape[2]
    pb, ka = lax.axis_index("pb"), lax.axis_index("ka")
    turn = lax.rem(pb + 1 + step, pb_size)
    peers = []
    for i in range(pb_size):
        for j in range(ka_size):
            if (i, j) != (pb_size - 1, 0):
                peers.append((lax.rem(pb + 1 + i, pb_size), lax.rem(ka + j, ka_size)))
    here_id = pb * ka_size + ka

    def term_copy(i, j):
        target = lax.rem(ka + j, ka_size)
        return push(
            dq_sent.at[i, target], dq_got.at[here_id], send_sems.at[i, j], recv_sems.at[i, j],
            (lax.rem(pb + 1 + i, pb_size), target),
        )

    blocks = chunk // LANES
    tiles = t_ref.shape[0] // LANES
    last_block = tiles - k_ref.shape[0] // LANES

    @pl.when(step == 0)
    def _():
        signal_peers(peers)
        build_table(w_ref, t_ref, tiles)
        g_ref[...] = jnp.zeros_like(g_ref)
        for kb in range(k_ref.shape[0] // key_rows):
            kt_ref[kb] = k_ref[kb * key_rows : (kb + 1) * key_rows, :].T
        dk_acc[...] = jnp.zeros_like(dk_acc)
        dv_acc[...] = jnp.zeros_like(dv_acc)

    @pl.when(step == 1)
    def _():
        await_peers(len(peers))

    @pl.when(step >= 1)
    def _():
        for j in range(ka_size):
            term_copy(step - 1, j).start()

    rows = jnp.concatenate([rows_ref[k % 2, k // 2, 0] for k in range(ka_size)], axis=0)
    lse_row, dots_row = stats_ref[0, 0:1, :], stats_ref[0, 1:2, :]
    q, g = rows[:, :dim], rows[:, dim:]
    dq_acc[...] = jnp.zeros_like(dq_acc)

    def one(kb, carry):
        at = kb * key_rows
        here = pl.ds(at, key_rows)
        scores = dot_nt(k_ref[here, :], q)
        dprobs = dot_nt(v_ref[here, :], g)
        probs_low, dscores_low = [], []
        for b in range(blocks):
            lanes = slice(b * LANES, (b + 1) * LANES)
            kappa = pl.multiple_of(at + LANES * (last_block - turn * blocks - b), LANES)
            there = pl.ds(kappa, key_rows)
            s = scores[:, lanes] * factor + t_ref[there, :]
            p = jnp.exp2(s - lse_row[:, lanes])
            ds = p * (dprobs[:, lanes] - dots_row[:, lanes])
            g_ref[there, :] = g_ref[there, :] + ds
            probs_low.append(p.astype(jnp.bfloat16))
            dscores_low.append(ds.astype(jnp.bfloat16))
        p_low = jnp.concatenate(probs_low, axis=1)
        ds_low = jnp.concatenate(dscores_low, axis=1)
        dv_acc[here, :] += dot_nn(p_low, g)
        dk_acc[here, :] += dot_nn(ds_low, q)
        dq_acc[...] += dot_nn(kt_ref[kb], ds_low)
        return carry

    for kb in range(k_ref.shape[0] // key_rows):
        one(kb, 0)

    width = dq_sent.shape[3]
    for b in range(ka_size):
        dq_sent[step, b] = dq_acc[:, b * width : (b + 1) * width].astype(dq_sent.dtype)

    @pl.when(step == pb_size - 1)
    def _():
        dk_ref[...] = (dk_acc[...] * scale).astype(dk_ref.dtype)
        dv_ref[...] = dv_acc[...].astype(dv_ref.dtype)
        for j in range(1, ka_size):
            term_copy(pb_size - 1, j).start()
        dq_got[here_id] = dq_sent[pb_size - 1, ka]
        fold_diagonals(g_ref, diag_ref, tiles)
        for i in range(pb_size):
            for j in range(ka_size):
                if (i, j) != (pb_size - 1, 0):
                    term_copy(i, j).wait()
        total = dq_got[0].astype(jnp.float32)
        for k in range(1, pb_size * ka_size):
            total = total + dq_got[k].astype(jnp.float32)
        dq_ref[...] = (total.T * scale).astype(dq_ref.dtype)


def backward(window, rows, stats, keys, values, factor, scale):
    cores, y_size, pb_size, part_rows, wide = rows.shape
    ka_size = cores * y_size
    count, dim = keys.shape[0] // pb_size, keys.shape[1]
    chunk = ka_size * part_rows
    tiles = count // LANES + pb_size * chunk // LANES - 1
    key_rows = min(256, count)
    whole = lambda i: (0, 0)
    f32 = jnp.float32

    def turn(i):
        return lax.rem(lax.axis_index("pb") + 1 + i, pb_size)

    return pl.pallas_call(
        lambda *refs: backward_kernel(key_rows, factor, scale, pb_size, ka_size, *refs),
        out_shape=(
            jax.ShapeDtypeStruct((part_rows, dim), jnp.bfloat16),
            jax.ShapeDtypeStruct((count, dim), jnp.bfloat16),
            jax.ShapeDtypeStruct((count, dim), jnp.bfloat16),
            jax.ShapeDtypeStruct(window.shape, f32),
        ),
        grid=(pb_size,),
        in_specs=[
            pl.BlockSpec(window.shape, whole),
            pl.BlockSpec((cores, y_size, 1, part_rows, wide), lambda i: (0, 0, turn(i), 0, 0)),
            pl.BlockSpec((1, 2, chunk), lambda i: (turn(i), 0, 0)),
            pl.BlockSpec((count, dim), lambda i: (lax.axis_index("pb"), 0)),
            pl.BlockSpec((count, dim), lambda i: (lax.axis_index("pb"), 0)),
        ],
        out_specs=(
            pl.BlockSpec((part_rows, dim), whole),
            pl.BlockSpec((count, dim), whole),
            pl.BlockSpec((count, dim), whole),
            pl.BlockSpec(window.shape, whole),
        ),
        scratch_shapes=[
            pltpu.VMEM((tiles * LANES, LANES), f32),
            pltpu.VMEM((tiles * LANES, LANES), f32),
            pltpu.VMEM((count, dim), f32),
            pltpu.VMEM((count, dim), f32),
            pltpu.VMEM((dim, chunk), f32),
            pltpu.VMEM((pb_size, ka_size, dim, part_rows), jnp.bfloat16),
            pltpu.VMEM((pb_size * ka_size, dim, part_rows), jnp.bfloat16),
            pltpu.VMEM((count // key_rows, dim, key_rows), jnp.bfloat16),
            dma((pb_size, ka_size)), dma((pb_size, ka_size)),
        ],
        compiler_params=pltpu.CompilerParams(collective_id=4, has_side_effects=True),
        name="backward",
    )(window, rows, stats, keys, values)


def hand_over(*arrays):
    def body(*refs):
        for source, target in zip(refs[: len(arrays)], refs[len(arrays) :]):
            target[...] = source[...]

    return pl.pallas_call(
        body,
        out_shape=tuple(jax.ShapeDtypeStruct(x.shape, x.dtype) for x in arrays),
        in_specs=[VMEM] * len(arrays),
        out_specs=tuple(VMEM for x in arrays),
        name="hand_over",
    )(*arrays)


def on_device(queries, keys, values, bias, grad_out, group_start):
    pb_size, ka_size = lax.axis_size("pb"), lax.axis_size("ka")
    pb, ka = lax.axis_index("pb"), lax.axis_index("ka")
    rows, dim = queries.shape
    key_count = keys.shape[0]
    total_rows = rows * pb_size
    scale = dim ** (-0.5)
    factor = scale * LOG2E
    first = group_start[0]

    part_rows = rows // ka_size
    both = jnp.concatenate([queries, grad_out], axis=1)
    own_rows = lax.dynamic_slice_in_dim(both, ka * part_rows, part_rows, 0)
    bias_all, pb_rows = entry_gather(bias.reshape(-1, LANES), own_rows, pb_size, ka_size)
    bias_all = bias_all.swapaxes(0, 1)

    bias_count = bias.shape[0] * pb_size * ka_size
    margin = key_count * ka_size
    tail = 2 * LANES
    table = jnp.concatenate(
        [
            jnp.full((margin,), NEGATIVE, jnp.float32),
            bias_all.reshape(-1) * LOG2E,
            jnp.zeros((tail,), jnp.float32),
        ]
    )

    def window_of(query_first, key_first, query_rows, key_rows):
        low = query_first - key_first - key_rows + 1 + margin
        size = key_rows + query_rows
        return low, lax.dynamic_slice_in_dim(table, low, size).reshape(-1, LANES)

    key_base = ka * key_count
    low, window = window_of(first + pb * rows, key_base, rows, key_count)
    stats, row_all = forward(
        window, queries, grad_out, keys, values, pb_rows, factor, pb_size, ka_size
    )

    own_count = key_count // pb_size
    low, window = window_of(first, key_base + pb * own_count, total_rows, own_count)
    query_grad, key_grad, value_grad, diag = backward(
        window, row_all, stats, keys, values, factor, scale
    )
    spread = lax.dynamic_update_slice_in_dim(
        jnp.zeros(table.shape, jnp.float32), diag.reshape(-1), low, 0
    )
    spread = spread[margin : margin + bias_count].reshape(pb_size, ka_size, -1, LANES)
    bias_grad = diagonal_reduce(spread)
    query_grad, key_grad, value_grad, bias_grad = hand_over(
        query_grad, key_grad, value_grad, bias_grad
    )
    return query_grad, key_grad, value_grad, bias_grad.reshape(-1)


def solution(mesh):
    return jax.shard_map(
        on_device,
        mesh=mesh,
        in_specs=(P("pb", None), P("ka", None), P("ka", None), P(("pb", "ka")), P("pb", None), P()),
        out_specs=(
            P(("pb", "ka"), None),
            P(("ka", "pb"), None),
            P(("ka", "pb"), None),
            P(("pb", "ka")),
        ),
        check_vma=False,
    )
```
